32 devices in a mesh: row: 8 (over z, y), leaf: 4 (over x, core).
Axes of the slice: x: 2, y: 2, z: 4, core: 2. Of those that a mesh axis runs over, the one named last changes fastest.
Arguments:
- leaf_index: int32 [8192, 256], P('row', 'leaf'), may hold values from 0 to 63
- targets: float32 [8192, 64], P('row'), may hold values from -6 to 6
Outputs:
- solution: float32 [16384, 64], P('leaf')
- residual: float32 [16384, 64], P('leaf')
The draws below stay inside these ranges and needn't reach their ends.
All inputs are finite; a program needn't handle non-finite values.
Results may differ from the reference program's by a relative error of at most 0.0003.
Values sent between devices are 32-bit elements; how exact they have to be, the bound alone decides.
No kernel may reach another device: no remote copies, remote signals or barrier semaphores. Data moves between devices by JAX's collectives and lax.ppermute only.
A program may use at most 64 MiB of HBM per device.

```python
import jax
import jax.numpy as jnp
from jax import lax

K = 64
LEAVES = 64
ITERS = 2
TREES = 256
ROWS = 8192
COLUMNS = 16384


def touch_ends(result, stream_key, least, largest):
    place = [jax.random.randint(jax.random.fold_in(stream_key, axis), (), 0, length) for axis, length in enumerate(result.shape)]
    longest = result.shape.index(max(result.shape))
    next_to = place[:longest] + [(place[longest] + 1) % result.shape[longest]] + place[longest + 1:]
    return result.at[tuple(place)].set(least).at[tuple(next_to)].set(largest)


def level_of(stream_key, shape, split, low, top_value):
    loudness = 1.0
    for position, blocks in split:
        draws = jax.random.uniform(jax.random.fold_in(jax.random.fold_in(stream_key, 6), position), (blocks,), jnp.float32, low / len(split), top_value / len(split))
        loudness = loudness * jnp.repeat(jnp.exp(draws), shape[position] // blocks).reshape((-1,) + (1,) * (len(shape) - 1 - position))
    return loudness


def bell_draw(own_key, extent, spread, reach, split=(), kind=jnp.bfloat16):
    entries = jax.random.normal(own_key, extent, jnp.float32) * spread
    if len(split) > 0:
        entries = level_of(own_key, extent, split, -0.22, 0.18) * entries
    return jnp.clip(entries, min=-reach, max=reach).astype(kind)


def setup_inputs(seed: int = 0) -> dict:
    key_of = jax.random.split(jax.random.key(seed), 3)
    leaf_index = touch_ends(jax.random.randint(key_of[0], (ROWS, TREES), 0, LEAVES), jax.random.fold_in(key_of[0], 1), 0, LEAVES - 1).astype(jnp.int32)
    targets = bell_draw(key_of[1], (ROWS, K), 1.0, 6.0, ((0, 8),), jnp.float32)
    return {"leaf_index": leaf_index, "targets": targets}


ridge_weight = 1.0


def forward(leaf_index, vector):
    tables = vector.reshape(TREES, LEAVES, K)

    def step(running, pair):
        indices, table = pair
        return running + table[indices], None

    start = jnp.zeros((ROWS, K), jnp.float32)
    running, _ = lax.scan(step, start, (leaf_index.T, tables))
    return running * (LEAVES / ROWS) ** 0.5


def backward(leaf_index, values):
    def step(carry, indices):
        return carry, jax.ops.segment_sum(values, indices, LEAVES)

    _, stacked = lax.scan(step, 0, leaf_index.T)
    return stacked.reshape(COLUMNS, K) * (LEAVES / ROWS) ** 0.5


def reference(leaf_index, targets):
    residual = backward(leaf_index, targets)
    solution = jnp.zeros_like(residual)
    direction = residual
    norm_now = jnp.sum(residual * residual)
    for step in range(ITERS):
        image = backward(leaf_index, forward(leaf_index, direction)) + ridge_weight * direction
        alpha = norm_now / jnp.sum(direction * image)
        solution = solution + alpha * direction
        residual = residual - alpha * image
        norm_next = jnp.sum(residual * residual)
        direction = residual + (norm_next / norm_now) * direction
        norm_now = norm_next
    return solution, residual
```

```python
import jax
import jax.numpy as jnp
from jax import lax
from jax.experimental import pallas as pl
from jax.experimental.pallas import tpu as pltpu
from jax.sharding import PartitionSpec as P


LEAVES = 64
LANES = 128
PIECES = 3
TREE_BLOCK = 16
ridge_weight = 1.0
F32, BF16 = jnp.float32, jnp.bfloat16
VMEM_LIMIT = 32 * 1024 * 1024
VMEM = pl.BlockSpec(memory_space=pltpu.VMEM)


def onehot(leaves):
    trees, rows = leaves.shape
    which = lax.broadcasted_iota(jnp.int32, (LEAVES, rows), 0).astype(F32).astype(BF16)
    leaves = leaves.astype(BF16)
    one, zero = jnp.ones((LEAVES, rows), BF16), jnp.zeros((LEAVES, rows), BF16)
    marks = [
        jnp.where(jnp.broadcast_to(leaves[t : t + 1, :], (LEAVES, rows)) == which, one, zero)
        for t in range(trees)
    ]
    return jnp.concatenate(marks, 0)


def pieces_of(value):
    found = []
    for _ in range(PIECES):
        high = value.astype(BF16)
        found.append(high)
        value = value - high.astype(F32)
    return jnp.concatenate(found, 0)


def pieces_sum(value):
    rows = value.shape[0] // PIECES
    total = value[(PIECES - 1) * rows :]
    for index in reversed(range(PIECES - 1)):
        total = total + value[index * rows : (index + 1) * rows]
    return total


def lane_sums(value):
    groups = [value[:, at : at + LANES] for at in range(0, value.shape[1], LANES)]
    while len(groups) > 1:
        groups = [sum(groups[at : at + 2]) for at in range(0, len(groups), 2)]
    return groups[0]


def call(kernel, outs, scratch, flops, *args):
    return pl.pallas_call(
        kernel,
        out_shape=outs,
        in_specs=[VMEM] * len(args),
        out_specs=jax.tree.map(lambda _: VMEM, outs),
        scratch_shapes=scratch,
        compiler_params=pltpu.CompilerParams(vmem_limit_bytes=VMEM_LIMIT),
        cost_estimate=pl.CostEstimate(flops=flops, bytes_accessed=1 << 20, transcendentals=0),
    )(*args)


def array(*shape):
    return jax.ShapeDtypeStruct(shape, F32)


def spread(leaf_refs, offsets, trees, split_ref, out_ref, scale, before=None):
    rows = leaf_refs[0].shape[1]

    @pl.loop(0, trees // TREE_BLOCK)
    def _(step):
        total = None
        for index, (leaf_ref, offset) in enumerate(zip(leaf_refs, offsets)):
            marks = onehot(leaf_ref[pl.ds(pl.multiple_of(offset + step * TREE_BLOCK, 8), TREE_BLOCK), :])
            part = lax.dot_general(
                split_ref[:, index * rows : (index + 1) * rows],
                marks,
                (((1,), (1,)), ((), ())),
                preferred_element_type=F32,
            )
            total = part if total is None else total + part
        width = TREE_BLOCK * LEAVES
        at = pl.ds(pl.multiple_of(step * width, width), width)
        result = scale * pieces_sum(total)
        out_ref[:, at] = result if before is None else before[:, at] + result


def collect(leaf_refs, offsets, trees, split_ref, out_ref, total_ref):
    rows = leaf_refs[0].shape[1]
    total_ref[...] = jnp.zeros_like(total_ref)

    @pl.loop(0, trees // TREE_BLOCK)
    def _(step):
        width = TREE_BLOCK * LEAVES
        split = split_ref[:, pl.ds(pl.multiple_of(step * width, width), width)]
        for index, (leaf_ref, offset) in enumerate(zip(leaf_refs, offsets)):
            marks = onehot(leaf_ref[pl.ds(pl.multiple_of(offset + step * TREE_BLOCK, 8), TREE_BLOCK), :])
            at = slice(index * rows, (index + 1) * rows)
            part = jnp.dot(split, marks, preferred_element_type=F32)
            total_ref[:, at] = total_ref[:, at] + part

    out_ref[:, : total_ref.shape[1]] = pieces_sum(total_ref[...])


def solution(mesh):
    n_row, n_leaf = mesh.shape["row"], mesh.shape["leaf"]
    far_stride, near_stride = n_row // 2, 1
    row_strides = [1 << bit for bit in range(1, n_row.bit_length() - 2)]
    leaf_strides = [1 << bit for bit in range(n_leaf.bit_length() - 1)]
    n_keys = 4
    n_share = n_row // n_keys

    def swap(value, axis, stride):
        size = n_row if axis == "row" else n_leaf
        return lax.ppermute(value, axis, [(i, i ^ stride) for i in range(size)])

    def gather(value):
        far = swap(value, "row", far_stride)
        near = swap(value, "row", near_stride)
        return [value, near, far, swap(far, "row", near_stride)]

    def half_sum(value, axis, strides):
        for stride in strides[:-1]:
            value = value + swap(value, axis, stride)
        return value, swap(value, axis, strides[-1])

    def per_device(leaf_index, targets):
        width = targets.shape[1] // n_keys
        rows, trees = leaf_index.shape
        columns, span = trees * LEAVES, n_keys * rows
        scale = (LEAVES / (rows * n_row)) ** 0.5
        flops = 2 * columns * rows * 256
        row = lax.axis_index("row")
        key = (row // far_stride) * 2 + row % 2
        place = jnp.stack([key, key ^ 1, key ^ 2, key ^ 3]).astype(jnp.int32)
        split_rows = pltpu.VMEM((PIECES * width, span), BF16)
        split_columns = pltpu.VMEM((PIECES * width, columns), BF16)

        def pack(place_ref, leaf_ref, target_ref, own_ref, near_ref, far_ref):
            leaves = leaf_ref[...].astype(F32)
            chunk = lambda m: target_ref[pl.ds(pl.multiple_of(place_ref[m] * width, width), width), :]
            own_ref[:trees, :] = leaves
            own_ref[trees:, :] = chunk(0)
            near_ref[:trees, :] = leaves
            near_ref[trees:, :] = chunk(1)
            far_ref[:width, :] = chunk(2)
            far_ref[width : width + trees, :] = leaves
            far_ref[width + trees :, :] = chunk(3)

        packed = array(trees + width, rows)
        own, near, far = pl.pallas_call(
            pack,
            out_shape=(packed, packed, array(trees + 2 * width, rows)),
            in_specs=[pl.BlockSpec(memory_space=pltpu.SMEM), VMEM, VMEM],
            out_specs=(VMEM, VMEM, VMEM),
            compiler_params=pltpu.CompilerParams(vmem_limit_bytes=VMEM_LIMIT),
            name="pack",
        )(place, leaf_index.T, targets.T)
        far = swap(far, "row", far_stride)
        near = swap(near, "row", near_stride)
        both = swap(far[width:], "row", near_stride)
        leaves, offsets = (own, near, far, both), (0, 0, width, 0)

        def first(own_ref, near_ref, out_ref, split_ref):
            for index, ref in enumerate((own_ref, near_ref)):
                split_ref[:, index * rows : (index + 1) * rows] = pieces_of(ref[trees:, :])
            spread((own_ref, near_ref), offsets[:2], trees, split_ref, out_ref, scale)

        def second(far_ref, both_ref, before_ref, out_ref, split_ref):
            split_ref[:, :rows] = pieces_of(far_ref[:width, :])
            split_ref[:, rows : 2 * rows] = pieces_of(both_ref[trees:, :])
            spread((far_ref, both_ref), offsets[2:], trees, split_ref, out_ref, scale, before_ref)

        b_shape = array(width, columns)
        part = call(first, b_shape, [split_rows], 2 * flops, own, near)
        part = call(second, b_shape, [split_rows], 2 * flops, far, both, part)
        mine, theirs = half_sum(part, "row", row_strides)

        def forward0(l0, l1, l2, l3, mine_ref, theirs_ref, out_ref, base_ref, split_ref, total_ref):
            base = mine_ref[...] + theirs_ref[...]
            base_ref[...] = base
            split_ref[...] = pieces_of(base)
            collect((l0, l1, l2, l3), offsets, trees, split_ref, out_ref, total_ref)
            out_ref[:, span:] = lane_sums(base * base)

        total_rows = pltpu.VMEM((PIECES * width, span), F32)
        part, b0 = call(
            forward0,
            (array(width, span + LANES), b_shape),
            [split_columns, total_rows],
            4 * flops,
            *leaves,
            mine,
            theirs,
        )
        mine, theirs = half_sum(part, "leaf", leaf_strides)

        def backward1(l0, l1, l2, l3, mine_ref, theirs_ref, out_ref, rows_ref, split_ref):
            value = mine_ref[:, :span] + theirs_ref[:, :span]
            rows_ref[...] = value
            split_ref[...] = pieces_of(value)
            out_ref[:, columns : columns + LANES] = (scale * scale) * lane_sums(value * value)
            out_ref[:, columns + LANES :] = (mine_ref[:, span:] + theirs_ref[:, span:]) * (1.0 / n_share)
            spread((l0, l1, l2, l3), offsets, trees, split_ref, out_ref, scale * scale)

        part, w0 = call(
            backward1,
            (array(width, columns + 2 * LANES), array(width, span)),
            [split_rows],
            4 * flops,
            *leaves,
            mine,
            theirs,
        )
        mine, theirs = half_sum(part, "row", row_strides)

        def step_of(norm, curve):
            return jnp.where(norm > 0.0, norm / (curve + ridge_weight * norm), 1.0)

        def scalar(value):
            return jnp.sum(value, axis=(0, 1), keepdims=True)

        def forward1(
            l0, l1, l2, l3, mine_ref, theirs_ref, base_ref, out_ref, res_ref, split_ref, total_ref
        ):
            tail = mine_ref[:, columns:] + theirs_ref[:, columns:]
            theta = step_of(scalar(tail[:, LANES:]), scalar(tail[:, :LANES]))
            base = base_ref[...]
            image = mine_ref[:, :columns] + theirs_ref[:, :columns] + ridge_weight * base
            res = base - theta * image
            res_ref[:, :columns] = res
            res_ref[:, columns:] = tail
            split_ref[...] = pieces_of(res)
            collect((l0, l1, l2, l3), offsets, trees, split_ref, out_ref, total_ref)
            out_ref[:, span : span + LANES] = lane_sums(res * res)
            out_ref[:, span + LANES :] = lane_sums(res * base)

        part, res = call(
            forward1,
            (array(width, span + 2 * LANES), array(width, columns + 2 * LANES)),
            [split_columns, total_rows],
            4 * flops,
            *leaves,
            mine,
            theirs,
            b0,
        )
        mine, theirs = half_sum(part, "leaf", leaf_strides)

        def backward2(l0, l1, l2, l3, mine_ref, theirs_ref, rows_ref, out_ref, split_ref):
            value = mine_ref[:, :span] + theirs_ref[:, :span]
            split_ref[...] = pieces_of(value)
            out_ref[:, columns : columns + LANES] = (scale * scale) * lane_sums(value * value)
            out_ref[:, columns + LANES : columns + 2 * LANES] = (scale * scale) * lane_sums(
                value * rows_ref[...]
            )
            out_ref[:, columns + 2 * LANES :] = (mine_ref[:, span:] + theirs_ref[:, span:]) * (
                1.0 / n_share
            )
            spread((l0, l1, l2, l3), offsets, trees, split_ref, out_ref, scale * scale)

        part = call(
            backward2,
            array(width, columns + 4 * LANES),
            [split_rows],
            4 * flops,
            *leaves,
            mine,
            theirs,
            w0,
        )
        mine, theirs = half_sum(part, "row", row_strides)
        b2 = mine + theirs

        def combine(place_ref, *refs):
            bases, ress, seconds = (refs[k * n_keys : (k + 1) * n_keys] for k in range(3))
            solution_ref, residual_ref = refs[3 * n_keys :]
            tail = lambda ref, at: scalar(ref[:, columns + at * LANES : columns + (at + 1) * LANES])
            keys = range(n_keys)
            b = [tail(ress[m], 0) for m in keys]
            a = [tail(ress[m], 1) for m in keys]
            e, f, c, d = ([tail(seconds[m], at) for m in keys] for at in range(4))
            norm0 = sum(a)
            alpha0 = norm0 / (sum(b) + ridge_weight * norm0)
            theta = [step_of(a[m], b[m]) for m in keys]
            rho = [alpha0 / theta[m] for m in keys]
            square = lambda x, y, xx, xy, yy: x * x * xx + 2.0 * x * y * xy + y * y * yy
            norm1 = sum(square(rho[m], 1.0 - rho[m], c[m], d[m], a[m]) for m in keys)
            beta = norm1 / norm0
            other = [1.0 - rho[m] + beta for m in keys]
            curve = sum(
                square(rho[m], other[m], e[m], f[m], b[m])
                + ridge_weight * square(rho[m], other[m], c[m], d[m], a[m])
                for m in keys
            )
            alpha1 = norm1 / curve
            for m in keys:
                at = pl.ds(pl.multiple_of(place_ref[m] * width, width), width)
                base, res, image = bases[m][...], ress[m][:, :columns], seconds[m][:, :columns]
                solution_ref[at, :] = (alpha0 + alpha1 * other[m]) * base + (alpha1 * rho[m]) * res
                residual_ref[at, :] = (
                    ((1.0 - rho[m]) - alpha1 * other[m] / theta[m]) * base
                    + (rho[m] + alpha1 * (other[m] / theta[m] - ridge_weight * rho[m])) * res
                    - (alpha1 * rho[m]) * image
                )

        out = array(n_keys * width, columns)
        result = pl.pallas_call(
            combine,
            out_shape=(out, out),
            in_specs=[pl.BlockSpec(memory_space=pltpu.SMEM)] + [VMEM] * (3 * n_keys),
            out_specs=(VMEM, VMEM),
            compiler_params=pltpu.CompilerParams(vmem_limit_bytes=VMEM_LIMIT),
            name="combine",
        )(place, *gather(b0), *gather(res), *gather(b2))
        return tuple(value.T for value in result)

    return jax.shard_map(
        per_device,
        mesh=mesh,
        in_specs=(P("row", "leaf"), P("row", None)),
        out_specs=(P("leaf", None), P("leaf", None)),
        check_vma=False,
    )
```

```python
import jax
import jax.numpy as jnp
from jax import lax
from jax.experimental import pallas as pl
from jax.experimental.pallas import tpu as pltpu
from jax.sharding import PartitionSpec as P


LEAVES = 64
LANES = 128
TREE_BLOCK = 32
ridge_weight = 1.0
F32, BF16, F8 = jnp.float32, jnp.bfloat16, jnp.float8_e4m3fn
VMEM_LIMIT = 32 * 1024 * 1024
VMEM = pl.BlockSpec(memory_space=pltpu.VMEM)


def onehot(leaves):
    trees, rows = leaves.shape
    which = lax.broadcasted_iota(jnp.int32, (LEAVES, rows), 0).astype(F32).astype(BF16)
    leaves = leaves.astype(BF16)
    one, zero = jnp.ones((LEAVES, rows), BF16), jnp.zeros((LEAVES, rows), BF16)
    marks = [
        jnp.where(jnp.broadcast_to(leaves[t : t + 1, :], (LEAVES, rows)) == which, one, zero)
        for t in range(trees)
    ]
    return jnp.concatenate(marks, 0).astype(F8)


WIDE, NARROW = (16.0, 6), (4.0, 12)
ROUND = 12582912.0


def top_of(value):
    return jnp.maximum(jnp.max(jnp.abs(value), axis=1, keepdims=True), 1e-30)


def digits_of(value, top, code):
    base, count = code
    value = value * (0.5 * base / top)
    found = []
    for _ in range(count):
        digit = (value + ROUND) - ROUND
        found.append(digit.astype(F8))
        value = (value - digit) * base
    return jnp.concatenate(found, 0)


def digits_sum(value, top, code):
    base, count = code
    rows = value.shape[0] // count
    total = value[(count - 1) * rows :]
    for index in reversed(range(count - 1)):
        total = value[index * rows : (index + 1) * rows] + total * (1.0 / base)
    return total * (top * (2.0 / base))


def lane_sums(value):
    groups = [value[:, at : at + LANES] for at in range(0, value.shape[1], LANES)]
    while len(groups) > 1:
        groups = [sum(groups[at : at + 2]) for at in range(0, len(groups), 2)]
    return groups[0]


def call(kernel, outs, scratch, flops, *args):
    return pl.pallas_call(
        kernel,
        out_shape=outs,
        in_specs=[VMEM] * len(args),
        out_specs=jax.tree.map(lambda _: VMEM, outs),
        scratch_shapes=scratch,
        compiler_params=pltpu.CompilerParams(vmem_limit_bytes=VMEM_LIMIT),
        cost_estimate=pl.CostEstimate(flops=flops, bytes_accessed=1 << 20, transcendentals=0),
    )(*args)


def array(*shape):
    return jax.ShapeDtypeStruct(shape, F32)


def spread(leaf_refs, offsets, trees, split_ref, top, out_ref, scale, before=None):
    rows = leaf_refs[0].shape[1]

    @pl.loop(0, trees // TREE_BLOCK)
    def _(step):
        total = None
        for index, (leaf_ref, offset) in enumerate(zip(leaf_refs, offsets)):
            marks = onehot(leaf_ref[pl.ds(pl.multiple_of(offset + step * TREE_BLOCK, 8), TREE_BLOCK), :])
            part = lax.dot_general(
                split_ref[:, index * rows : (index + 1) * rows],
                marks,
                (((1,), (1,)), ((), ())),
                preferred_element_type=F32,
            )
            total = part if total is None else total + part
        width = TREE_BLOCK * LEAVES
        at = pl.ds(pl.multiple_of(step * width, width), width)
        result = digits_sum(total, scale * top, NARROW)
        out_ref[:, at] = result if before is None else before[:, at] + result


def collect(leaf_refs, offsets, trees, split_ref, top, out_ref, total_ref):
    rows = leaf_refs[0].shape[1]
    total_ref[...] = jnp.zeros_like(total_ref)

    @pl.loop(0, trees // TREE_BLOCK)
    def _(step):
        width = TREE_BLOCK * LEAVES
        split = split_ref[:, pl.ds(pl.multiple_of(step * width, width), width)]
        for index, (leaf_ref, offset) in enumerate(zip(leaf_refs, offsets)):
            marks = onehot(leaf_ref[pl.ds(pl.multiple_of(offset + step * TREE_BLOCK, 8), TREE_BLOCK), :])
            at = slice(index * rows, (index + 1) * rows)
            part = jnp.dot(split, marks, preferred_element_type=F32)
            total_ref[:, at] = total_ref[:, at] + part

    out_ref[:, : total_ref.shape[1]] = digits_sum(total_ref[...], top, WIDE)


def solution(mesh):
    n_row, n_leaf = mesh.shape["row"], mesh.shape["leaf"]
    far_stride, near_stride = n_row // 2, 1
    row_strides = [1 << bit for bit in range(1, n_row.bit_length() - 2)]
    leaf_strides = [1 << bit for bit in range(n_leaf.bit_length() - 1)]
    n_keys = 4
    n_share = n_row // n_keys

    def swap(value, axis, stride):
        size = n_row if axis == "row" else n_leaf
        return lax.ppermute(value, axis, [(i, i ^ stride) for i in range(size)])

    def gather(value):
        far = swap(value, "row", far_stride)
        near = swap(value, "row", near_stride)
        return [value, near, far, swap(far, "row", near_stride)]

    def half_sum(value, axis, strides):
        for stride in strides[:-1]:
            value = value + swap(value, axis, stride)
        return value, swap(value, axis, strides[-1])

    def per_device(leaf_index, targets):
        width = targets.shape[1] // n_keys
        rows, trees = leaf_index.shape
        columns, span = trees * LEAVES, n_keys * rows
        scale = (LEAVES / (rows * n_row)) ** 0.5
        flops = 2 * columns * rows * 256
        row = lax.axis_index("row")
        key = (row // far_stride) * 2 + row % 2
        place = jnp.stack([key, key ^ 1, key ^ 2, key ^ 3]).astype(jnp.int32)
        split_rows = pltpu.VMEM((NARROW[1] * width, span), F8)
        split_columns = pltpu.VMEM((WIDE[1] * width, columns), F8)

        def pack(place_ref, leaf_ref, target_ref, own_ref, near_ref, far_ref):
            leaves = leaf_ref[...].astype(F32)
            chunk = lambda m: target_ref[pl.ds(pl.multiple_of(place_ref[m] * width, width), width), :]
            own_ref[:trees, :] = leaves
            own_ref[trees:, :] = chunk(0)
            near_ref[:trees, :] = leaves
            near_ref[trees:, :] = chunk(1)
            far_ref[:width, :] = chunk(2)
            far_ref[width : width + trees, :] = leaves
            far_ref[width + trees :, :] = chunk(3)

        packed = array(trees + width, rows)
        own, near, far = pl.pallas_call(
            pack,
            out_shape=(packed, packed, array(trees + 2 * width, rows)),
            in_specs=[pl.BlockSpec(memory_space=pltpu.SMEM), VMEM, VMEM],
            out_specs=(VMEM, VMEM, VMEM),
            compiler_params=pltpu.CompilerParams(vmem_limit_bytes=VMEM_LIMIT),
            name="pack",
        )(place, leaf_index.T, targets.T)
        far = swap(far, "row", far_stride)
        near = swap(near, "row", near_stride)
        both = swap(far[width:], "row", near_stride)
        leaves, offsets = (own, near, far, both), (0, 0, width, 0)

        def first(own_ref, near_ref, out_ref, split_ref):
            chunks = own_ref[trees:, :], near_ref[trees:, :]
            top = jnp.maximum(top_of(chunks[0]), top_of(chunks[1]))
            for index, chunk in enumerate(chunks):
                split_ref[:, index * rows : (index + 1) * rows] = digits_of(chunk, top, NARROW)
            spread((own_ref, near_ref), offsets[:2], trees, split_ref, top, out_ref, scale)

        def second(far_ref, both_ref, before_ref, out_ref, split_ref):
            chunks = far_ref[:width, :], both_ref[trees:, :]
            top = jnp.maximum(top_of(chunks[0]), top_of(chunks[1]))
            for index, chunk in enumerate(chunks):
                split_ref[:, index * rows : (index + 1) * rows] = digits_of(chunk, top, NARROW)
            spread((far_ref, both_ref), offsets[2:], trees, split_ref, top, out_ref, scale, before_ref)

        b_shape = array(width, columns)
        part = call(first, b_shape, [split_rows], 2 * flops, own, near)
        part = call(second, b_shape, [split_rows], 2 * flops, far, both, part)
        mine, theirs = half_sum(part, "row", row_strides)

        def forward0(l0, l1, l2, l3, mine_ref, theirs_ref, out_ref, base_ref, split_ref, total_ref):
            base = mine_ref[...] + theirs_ref[...]
            base_ref[...] = base
            top = top_of(base)
            split_ref[...] = digits_of(base, top, WIDE)
            collect((l0, l1, l2, l3), offsets, trees, split_ref, top, out_ref, total_ref)
            out_ref[:, span:] = lane_sums(base * base)

        total_rows = pltpu.VMEM((WIDE[1] * width, span), F32)
        part, b0 = call(
            forward0,
            (array(width, span + LANES), b_shape),
            [split_columns, total_rows],
            4 * flops,
            *leaves,
            mine,
            theirs,
        )
        mine, theirs = half_sum(part, "leaf", leaf_strides)

        def backward1(l0, l1, l2, l3, mine_ref, theirs_ref, out_ref, rows_ref, split_ref):
            value = mine_ref[:, :span] + theirs_ref[:, :span]
            rows_ref[...] = value
            top = top_of(value)
            split_ref[...] = digits_of(value, top, NARROW)
            out_ref[:, columns : columns + LANES] = (scale * scale) * lane_sums(value * value)
            out_ref[:, columns + LANES :] = (mine_ref[:, span:] + theirs_ref[:, span:]) * (1.0 / n_share)
            spread((l0, l1, l2, l3), offsets, trees, split_ref, top, out_ref, scale * scale)

        part, w0 = call(
            backward1,
            (array(width, columns + 2 * LANES), array(width, span)),
            [split_rows],
            4 * flops,
            *leaves,
            mine,
            theirs,
        )
        mine, theirs = half_sum(part, "row", row_strides)

        def step_of(norm, curve):
            return jnp.where(norm > 0.0, norm / (curve + ridge_weight * norm), 1.0)

        def scalar(value):
            return jnp.sum(value, axis=(0, 1), keepdims=True)

        def forward1(
            l0, l1, l2, l3, mine_ref, theirs_ref, base_ref, out_ref, res_ref, split_ref, total_ref
        ):
            tail = mine_ref[:, columns:] + theirs_ref[:, columns:]
            theta = step_of(scalar(tail[:, LANES:]), scalar(tail[:, :LANES]))
            base = base_ref[...]
            image = mine_ref[:, :columns] + theirs_ref[:, :columns] + ridge_weight * base
            res = base - theta * image
            res_ref[:, :columns] = res
            res_ref[:, columns:] = tail
            top = top_of(res)
            split_ref[...] = digits_of(res, top, WIDE)
            collect((l0, l1, l2, l3), offsets, trees, split_ref, top, out_ref, total_ref)
            out_ref[:, span : span + LANES] = lane_sums(res * res)
            out_ref[:, span + LANES :] = lane_sums(res * base)

        part, res = call(
            forward1,
            (array(width, span + 2 * LANES), array(width, columns + 2 * LANES)),
            [split_columns, total_rows],
            4 * flops,
            *leaves,
            mine,
            theirs,
            b0,
        )
        mine, theirs = half_sum(part, "leaf", leaf_strides)

        def backward2(l0, l1, l2, l3, mine_ref, theirs_ref, rows_ref, out_ref, split_ref):
            value = mine_ref[:, :span] + theirs_ref[:, :span]
            top = top_of(value)
            split_ref[...] = digits_of(value, top, NARROW)
            out_ref[:, columns : columns + LANES] = (scale * scale) * lane_sums(value * value)
            out_ref[:, columns + LANES : columns + 2 * LANES] = (scale * scale) * lane_sums(
                value * rows_ref[...]
            )
            out_ref[:, columns + 2 * LANES :] = (mine_ref[:, span:] + theirs_ref[:, span:]) * (
                1.0 / n_share
            )
            spread((l0, l1, l2, l3), offsets, trees, split_ref, top, out_ref, scale * scale)

        part = call(
            backward2,
            array(width, columns + 4 * LANES),
            [split_rows],
            4 * flops,
            *leaves,
            mine,
            theirs,
            w0,
        )
        mine, theirs = half_sum(part, "row", row_strides)
        b2 = mine + theirs

        def combine(place_ref, *refs):
            bases, ress, seconds = (refs[k * n_keys : (k + 1) * n_keys] for k in range(3))
            solution_ref, residual_ref = refs[3 * n_keys :]
            tail = lambda ref, at: scalar(ref[:, columns + at * LANES : columns + (at + 1) * LANES])
            keys = range(n_keys)
            b = [tail(ress[m], 0) for m in keys]
            a = [tail(ress[m], 1) for m in keys]
            e, f, c, d = ([tail(seconds[m], at) for m in keys] for at in range(4))
            norm0 = sum(a)
            alpha0 = norm0 / (sum(b) + ridge_weight * norm0)
            theta = [step_of(a[m], b[m]) for m in keys]
            rho = [alpha0 / theta[m] for m in keys]
            square = lambda x, y, xx, xy, yy: x * x * xx + 2.0 * x * y * xy + y * y * yy
            norm1 = sum(square(rho[m], 1.0 - rho[m], c[m], d[m], a[m]) for m in keys)
            beta = norm1 / norm0
            other = [1.0 - rho[m] + beta for m in keys]
            curve = sum(
                square(rho[m], other[m], e[m], f[m], b[m])
                + ridge_weight * square(rho[m], other[m], c[m], d[m], a[m])
                for m in keys
            )
            alpha1 = norm1 / curve
            for m in keys:
                at = pl.ds(pl.multiple_of(place_ref[m] * width, width), width)
                base, res, image = bases[m][...], ress[m][:, :columns], seconds[m][:, :columns]
                solution_ref[at, :] = (alpha0 + alpha1 * other[m]) * base + (alpha1 * rho[m]) * res
                residual_ref[at, :] = (
                    ((1.0 - rho[m]) - alpha1 * other[m] / theta[m]) * base
                    + (rho[m] + alpha1 * (other[m] / theta[m] - ridge_weight * rho[m])) * res
                    - (alpha1 * rho[m]) * image
                )

        out = array(n_keys * width, columns)
        result = pl.pallas_call(
            combine,
            out_shape=(out, out),
            in_specs=[pl.BlockSpec(memory_space=pltpu.SMEM)] + [VMEM] * (3 * n_keys),
            out_specs=(VMEM, VMEM),
            compiler_params=pltpu.CompilerParams(vmem_limit_bytes=VMEM_LIMIT),
            name="combine",
        )(place, *gather(b0), *gather(res), *gather(b2))
        return tuple(value.T for value in result)

    return jax.shard_map(
        per_device,
        mesh=mesh,
        in_specs=(P("row", "leaf"), P("row", None)),
        out_specs=(P("leaf", None), P("leaf", None)),
        check_vma=False,
    )
```

```python
import jax
import jax.numpy as jnp
from jax import lax
from jax.experimental import pallas as pl
from jax.experimental.pallas import tpu as pltpu
from jax.sharding import PartitionSpec as P


LEAVES = 64
LANES = 128
ridge_weight = 1.0
F32, BF16, F8 = jnp.float32, jnp.bfloat16, jnp.float8_e4m3fn
VMEM_LIMIT = 32 * 1024 * 1024
VMEM = pl.BlockSpec(memory_space=pltpu.VMEM)


def onehot(leaves):
    trees, rows = leaves.shape
    which = lax.broadcasted_iota(jnp.int32, (LEAVES, rows), 0).astype(F32).astype(BF16)
    leaves = leaves.astype(F32).astype(BF16)
    one, zero = jnp.ones((LEAVES, rows), BF16), jnp.zeros((LEAVES, rows), BF16)
    marks = [
        jnp.where(jnp.broadcast_to(leaves[t : t + 1, :], (LEAVES, rows)) == which, one, zero)
        for t in range(trees)
    ]
    return jnp.concatenate(marks, 0).astype(F8)


WIDE, NARROW = (16.0, 6), (4.0, 12)
ROUND = 12582912.0


def top_of(value):
    return jnp.maximum(jnp.max(jnp.abs(value), axis=1, keepdims=True), 1e-30)


def digits_of(value, top, code):
    base, count = code
    value = value * (0.5 * base / top)
    found = []
    for _ in range(count):
        digit = (value + ROUND) - ROUND
        found.append(digit.astype(F8))
        value = (value - digit) * base
    return jnp.concatenate(found, 0)


def digits_sum(value, top, code):
    base, count = code
    rows = value.shape[0] // count
    total = value[(count - 1) * rows :]
    for index in reversed(range(count - 1)):
        total = value[index * rows : (index + 1) * rows] + total * (1.0 / base)
    return total * (top * (2.0 / base))


def lane_sums(value):
    groups = [value[:, at : at + LANES] for at in range(0, value.shape[1], LANES)]
    while len(groups) > 1:
        groups = [sum(groups[at : at + 2]) for at in range(0, len(groups), 2)]
    return groups[0]


def call(kernel, outs, scratch, flops, *args):
    return pl.pallas_call(
        kernel,
        out_shape=outs,
        in_specs=[VMEM] * len(args),
        out_specs=jax.tree.map(lambda _: VMEM, outs),
        scratch_shapes=scratch,
        compiler_params=pltpu.CompilerParams(vmem_limit_bytes=VMEM_LIMIT),
        cost_estimate=pl.CostEstimate(flops=flops, bytes_accessed=1 << 20, transcendentals=0),
    )(*args)


def array(*shape):
    return jax.ShapeDtypeStruct(shape, F32)


def spread(blocks, split_ref, top, scale):
    total, at = None, 0
    for ref, start, trees in blocks:
        rows = ref.shape[1]
        part = lax.dot_general(
            split_ref[:, at : at + rows],
            onehot(ref[start : start + trees, :]),
            (((1,), (1,)), ((), ())),
            preferred_element_type=F32,
        )
        total = part if total is None else total + part
        at += rows
    return digits_sum(total, scale * top, NARROW)


def collect(blocks, vector, out_ref, before_ref):
    top = top_of(vector)
    split = digits_of(vector, top, WIDE)
    at = 0
    for ref, start, trees in blocks:
        rows = ref.shape[1]
        part = jnp.dot(split, onehot(ref[start : start + trees, :]), preferred_element_type=F32)
        part = digits_sum(part, top, WIDE)
        if before_ref is not None:
            part = part + before_ref[:, at : at + rows]
        out_ref[:, at : at + rows] = part
        at += rows


def solution(mesh):
    n_row, n_leaf = mesh.shape["row"], mesh.shape["leaf"]
    far_stride, near_stride = n_row // 2, 1
    row_strides = [1 << bit for bit in range(1, n_row.bit_length() - 2)]
    leaf_strides = [1 << bit for bit in range(n_leaf.bit_length() - 1)]
    n_keys = 4
    n_share = n_row // n_keys

    def swap(value, axis, stride):
        size = n_row if axis == "row" else n_leaf
        return lax.ppermute(value, axis, [(i, i ^ stride) for i in range(size)])

    def far_swap(value):
        return swap(value, "row", far_stride)

    def near_swap(value):
        return swap(value, "row", near_stride)

    def gather(value):
        far = far_swap(value)
        near = near_swap(value)
        return [value, near, far, near_swap(far)]

    def half_sum(value, axis, strides):
        for stride in strides[:-1]:
            value = value + swap(value, axis, stride)
        return value, swap(value, axis, strides[-1])

    def per_device(leaf_index, targets):
        width = targets.shape[1] // n_keys
        rows, trees = leaf_index.shape
        half = trees // 2
        columns, span = half * LEAVES, n_keys * rows
        scale = (LEAVES / (rows * n_row)) ** 0.5
        flops = 2 * columns * rows * 256
        row = lax.axis_index("row")
        key = (row // far_stride) * 2 + row % 2
        place = jnp.stack([key, key ^ 1, key ^ 2, key ^ 3]).astype(jnp.int32)

        def pack(place_ref, target_ref, own_ref, near_ref, far_ref):
            chunk = lambda m: target_ref[pl.ds(pl.multiple_of(place_ref[m] * width, width), width), :]
            own_ref[...] = chunk(0)
            near_ref[...] = chunk(1)
            far_ref[:width, :] = chunk(2)
            far_ref[width:, :] = chunk(3)

        own = leaf_index.T
        t_own, t_near, t_far = pl.pallas_call(
            pack,
            out_shape=(array(width, rows), array(width, rows), array(2 * width, rows)),
            in_specs=[pl.BlockSpec(memory_space=pltpu.SMEM), VMEM],
            out_specs=(VMEM, VMEM, VMEM),
            compiler_params=pltpu.CompilerParams(vmem_limit_bytes=VMEM_LIMIT),
            name="pack",
        )(place, targets.T)
        far = [far_swap(own[:half]), far_swap(own[half:])]
        t_far = far_swap(t_far)
        near = near_swap(own)
        t_near = near_swap(t_near)
        both = [near_swap(far[0]), near_swap(far[1])]
        t_both = near_swap(t_far[width:])

        def leaves_of(h):
            return own, near, far[h], both[h]

        def blocks_of(refs, h):
            return tuple((ref, start, half) for ref, start in zip(refs, (h * half, h * half, 0, 0)))

        split_two = pltpu.VMEM((NARROW[1] * width, 2 * rows), F8)
        split_one = pltpu.VMEM((NARROW[1] * width, rows), F8)

        def back0_own(own_ref, near_ref, first_ref, second_ref, out0_ref, out1_ref, split_ref):
            chunks = first_ref[...], second_ref[...]
            top = jnp.maximum(top_of(chunks[0]), top_of(chunks[1]))
            for index, chunk in enumerate(chunks):
                split_ref[:, index * rows : (index + 1) * rows] = digits_of(chunk, top, NARROW)
            for h, ref in enumerate((out0_ref, out1_ref)):
                ref[...] = spread(blocks_of((own_ref, near_ref), h), split_ref, top, scale)

        def back0_far(far0_ref, far1_ref, value_ref, in0_ref, in1_ref, out0_ref, out1_ref, split_ref):
            value = value_ref[:width, :]
            top = top_of(value)
            split_ref[...] = digits_of(value, top, NARROW)
            out0_ref[...] = in0_ref[...] + spread(((far0_ref, 0, half),), split_ref, top, scale)
            out1_ref[...] = in1_ref[...] + spread(((far1_ref, 0, half),), split_ref, top, scale)

        def back0_both(leaf_ref, value_ref, in_ref, out_ref, split_ref):
            value = value_ref[...]
            top = top_of(value)
            split_ref[...] = digits_of(value, top, NARROW)
            out_ref[...] = in_ref[...] + spread(((leaf_ref, 0, half),), split_ref, top, scale)

        b_half = array(width, columns)
        parts = call(back0_own, (b_half, b_half), [split_two], 4 * flops, own, near, t_own, t_near)
        parts = call(back0_far, (b_half, b_half), [split_one], 2 * flops, *far, t_far, *parts)
        pairs = []
        for h in range(2):
            part = call(back0_both, b_half, [split_one], flops, both[h], t_both, parts[h])
            pairs.append(half_sum(part, "row", row_strides))

        w_shape = array(width, span + LANES)

        def forward0_first(l0, l1, l2, l3, mine_ref, theirs_ref, out_ref, base_ref):
            base = mine_ref[...] + theirs_ref[...]
            base_ref[...] = base
            collect(blocks_of((l0, l1, l2, l3), 0), base, out_ref, None)
            out_ref[:, span:] = lane_sums(base * base)

        def forward0_second(l0, l1, l2, l3, mine_ref, theirs_ref, in_ref, first_ref, out_ref, base_ref):
            base = mine_ref[...] + theirs_ref[...]
            base_ref[:, :columns] = first_ref[...]
            base_ref[:, columns:] = base
            collect(blocks_of((l0, l1, l2, l3), 1), base, out_ref, in_ref)
            out_ref[:, span:] = in_ref[:, span:] + lane_sums(base * base)

        part, first = call(forward0_first, (w_shape, b_half), [], 4 * flops, *leaves_of(0), *pairs[0])
        part, b0 = call(
            forward0_second, (w_shape, array(width, 2 * columns)), [], 4 * flops, *leaves_of(1), *pairs[1], part, first
        )
        w_pair = half_sum(part, "leaf", leaf_strides)

        split_shape = jax.ShapeDtypeStruct((NARROW[1] * width, span), F8)
        top_shape = array(width, 1)

        def backward_first(l0, l1, l2, l3, mine_ref, theirs_ref, *refs):
            rows_ref, (out_ref, split_ref, top_ref, last_ref) = refs[:-4], refs[-4:]
            value = mine_ref[:, :span] + theirs_ref[:, :span]
            if not rows_ref:
                last_ref[...] = value
            top = top_of(value)
            top_ref[...] = top
            split_ref[...] = digits_of(value, top, NARROW)
            tail = [value * value] + [value * ref[...] for ref in rows_ref]
            at = columns
            for product in tail:
                out_ref[:, at : at + LANES] = (scale * scale) * lane_sums(product)
                at += LANES
            out_ref[:, at:] = (mine_ref[:, span:] + theirs_ref[:, span:]) * (1.0 / n_share)
            out_ref[:, :columns] = spread(
                blocks_of((l0, l1, l2, l3), 0), split_ref, top, scale * scale
            )
            if rows_ref:
                last_ref[...] = jnp.zeros_like(last_ref)

        def backward_second(l0, l1, l2, l3, split_ref, top_ref, out_ref):
            out_ref[...] = spread(blocks_of((l0, l1, l2, l3), 1), split_ref, top_ref[...], scale * scale)

        def backward(w_pair, extra, *rows_before):
            part, split, top, last = call(
                backward_first,
                (
                    array(width, columns + extra * LANES),
                    split_shape,
                    top_shape,
                    array(8, LANES) if rows_before else array(width, span),
                ),
                [],
                4 * flops,
                *leaves_of(0),
                *w_pair,
                *rows_before,
            )
            pairs = [half_sum(part, "row", row_strides)]
            part = call(backward_second, b_half, [], 4 * flops, *leaves_of(1), split, top)
            return pairs + [half_sum(part, "row", row_strides)], last

        pairs, w0 = backward(w_pair, 2)

        def step_of(norm, curve):
            return jnp.where(norm > 0.0, norm / (curve + ridge_weight * norm), 1.0)

        def scalar(value):
            return jnp.sum(value, axis=(0, 1), keepdims=True)

        def theta_of(tail):
            return step_of(scalar(tail[:, LANES:]), scalar(tail[:, :LANES]))

        def residual(base, mine_ref, theirs_ref, theta):
            image = mine_ref[:, :columns] + theirs_ref[:, :columns]
            return base - theta * (image + ridge_weight * base)

        def forward1_first(l0, l1, l2, l3, mine_ref, theirs_ref, base_ref, out_ref, res_ref):
            tail = mine_ref[:, columns:] + theirs_ref[:, columns:]
            base = base_ref[:, :columns]
            res = residual(base, mine_ref, theirs_ref, theta_of(tail))
            res_ref[:, :columns] = res
            res_ref[:, columns:] = tail
            collect(blocks_of((l0, l1, l2, l3), 0), res, out_ref, None)
            out_ref[:, span : span + LANES] = lane_sums(res * res)
            out_ref[:, span + LANES :] = lane_sums(res * base)

        def forward1_second(
            l0, l1, l2, l3, mine_ref, theirs_ref, base_ref, in_ref, first_ref, out_ref, res_ref
        ):
            tail = first_ref[:, columns:]
            base = base_ref[:, columns:]
            res = residual(base, mine_ref, theirs_ref, theta_of(tail))
            res_ref[:, :columns] = first_ref[:, :columns]
            res_ref[:, columns : 2 * columns] = res
            res_ref[:, 2 * columns :] = tail
            collect(blocks_of((l0, l1, l2, l3), 1), res, out_ref, in_ref)
            out_ref[:, span : span + LANES] = in_ref[:, span : span + LANES] + lane_sums(res * res)
            out_ref[:, span + LANES :] = in_ref[:, span + LANES :] + lane_sums(res * base)

        w_shape = array(width, span + 2 * LANES)
        part, first = call(
            forward1_first, (w_shape, array(width, columns + 2 * LANES)), [], 4 * flops, *leaves_of(0), *pairs[0], b0
        )
        part, res = call(
            forward1_second,
            (w_shape, array(width, 2 * columns + 2 * LANES)),
            [],
            4 * flops,
            *leaves_of(1),
            *pairs[1],
            b0,
            part,
            first,
        )
        w_pair = half_sum(part, "leaf", leaf_strides)

        pairs, _ = backward(w_pair, 4, w0)
        b2 = [mine + theirs for mine, theirs in pairs]

        def combine(place_ref, *refs):
            bases, ress, firsts, seconds = (refs[k * n_keys : (k + 1) * n_keys] for k in range(4))
            solution_ref, residual_ref = refs[4 * n_keys :]

            def tail(ref, start, at):
                return scalar(ref[:, start + at * LANES : start + (at + 1) * LANES])

            keys = range(n_keys)
            b = [tail(ress[m], 2 * columns, 0) for m in keys]
            a = [tail(ress[m], 2 * columns, 1) for m in keys]
            e, f, c, d = ([tail(firsts[m], columns, at) for m in keys] for at in range(4))
            norm0 = sum(a)
            alpha0 = norm0 / (sum(b) + ridge_weight * norm0)
            theta = [step_of(a[m], b[m]) for m in keys]
            rho = [alpha0 / theta[m] for m in keys]
            square = lambda x, y, xx, xy, yy: x * x * xx + 2.0 * x * y * xy + y * y * yy
            norm1 = sum(square(rho[m], 1.0 - rho[m], c[m], d[m], a[m]) for m in keys)
            beta = norm1 / norm0
            other = [1.0 - rho[m] + beta for m in keys]
            curve = sum(
                square(rho[m], other[m], e[m], f[m], b[m])
                + ridge_weight * square(rho[m], other[m], c[m], d[m], a[m])
                for m in keys
            )
            alpha1 = norm1 / curve
            for m in keys:
                at = pl.ds(pl.multiple_of(place_ref[m] * width, width), width)
                for h, images in enumerate((firsts, seconds)):
                    of_half = slice(h * columns, (h + 1) * columns)
                    base, res, image = bases[m][:, of_half], ress[m][:, of_half], images[m][:, :columns]
                    solution_ref[at, of_half] = (alpha0 + alpha1 * other[m]) * base + (
                        alpha1 * rho[m]
                    ) * res
                    residual_ref[at, of_half] = (
                        ((1.0 - rho[m]) - alpha1 * other[m] / theta[m]) * base
                        + (rho[m] + alpha1 * (other[m] / theta[m] - ridge_weight * rho[m])) * res
                        - (alpha1 * rho[m]) * image
                    )

        out = array(n_keys * width, 2 * columns)
        result = pl.pallas_call(
            combine,
            out_shape=(out, out),
            in_specs=[pl.BlockSpec(memory_space=pltpu.SMEM)] + [VMEM] * (4 * n_keys),
            out_specs=(VMEM, VMEM),
            compiler_params=pltpu.CompilerParams(vmem_limit_bytes=VMEM_LIMIT),
            name="combine",
        )(place, *gather(b0), *gather(res), *gather(b2[0]), *gather(b2[1]))
        return tuple(value.T for value in result)

    return jax.shard_map(
        per_device,
        mesh=mesh,
        in_specs=(P("row", "leaf"), P("row", None)),
        out_specs=(P("leaf", None), P("leaf", None)),
        check_vma=False,
    )
```

```python
import jax
import jax.numpy as jnp
from jax import lax
from jax.experimental import pallas as pl
from jax.experimental.pallas import tpu as pltpu
from jax.sharding import PartitionSpec as P


LEAVES = 64
LANES = 128
ridge_weight = 1.0
F32, BF16, F8 = jnp.float32, jnp.bfloat16, jnp.float8_e4m3fn
VMEM_LIMIT = 32 * 1024 * 1024
VMEM = pl.BlockSpec(memory_space=pltpu.VMEM)


def onehot(leaves):
    trees, rows = leaves.shape
    which = lax.broadcasted_iota(jnp.int32, (LEAVES, rows), 0).astype(F32).astype(BF16)
    leaves = leaves.astype(F32).astype(BF16)
    one, zero = jnp.ones((LEAVES, rows), BF16), jnp.zeros((LEAVES, rows), BF16)
    marks = [
        jnp.where(jnp.broadcast_to(leaves[t : t + 1, :], (LEAVES, rows)) == which, one, zero)
        for t in range(trees)
    ]
    return jnp.concatenate(marks, 0).astype(F8)


WIDE, NARROW = (16.0, 6), (4.0, 12)
ROUND = 12582912.0


def top_of(value):
    return jnp.maximum(jnp.max(jnp.abs(value), axis=1, keepdims=True), 1e-30)


def digits_of(value, top, code):
    base, count = code
    value = value * (0.5 * base / top)
    found = []
    for _ in range(count):
        digit = (value + ROUND) - ROUND
        found.append(digit.astype(F8))
        value = (value - digit) * base
    return jnp.concatenate(found, 0)


def digits_sum(value, top, code):
    base, count = code
    rows = value.shape[0] // count
    total = value[(count - 1) * rows :]
    for index in reversed(range(count - 1)):
        total = value[index * rows : (index + 1) * rows] + total * (1.0 / base)
    return total * (top * (2.0 / base))


def lane_sums(value):
    groups = [value[:, at : at + LANES] for at in range(0, value.shape[1], LANES)]
    while len(groups) > 1:
        groups = [sum(groups[at : at + 2]) for at in range(0, len(groups), 2)]
    return groups[0]


def call(kernel, outs, scratch, flops, *args):
    return pl.pallas_call(
        kernel,
        out_shape=outs,
        in_specs=[VMEM] * len(args),
        out_specs=jax.tree.map(lambda _: VMEM, outs),
        scratch_shapes=scratch,
        compiler_params=pltpu.CompilerParams(vmem_limit_bytes=VMEM_LIMIT),
        cost_estimate=pl.CostEstimate(flops=flops, bytes_accessed=1 << 20, transcendentals=0),
    )(*args)


def array(*shape):
    return jax.ShapeDtypeStruct(shape, F32)


def spread(blocks, split_ref, top, scale):
    total, at = None, 0
    for ref, start, trees in blocks:
        rows = ref.shape[1]
        part = lax.dot_general(
            split_ref[:, at : at + rows],
            onehot(ref[start : start + trees, :]),
            (((1,), (1,)), ((), ())),
            preferred_element_type=F32,
        )
        total = part if total is None else total + part
        at += rows
    return digits_sum(total, scale * top, NARROW)


def collect(blocks, vector, out_ref, before_ref):
    top = top_of(vector)
    split = digits_of(vector, top, WIDE)
    for index, (ref, start, trees) in enumerate(blocks):
        rows = ref.shape[1]
        at = index * rows + (0 if index < 2 else out_ref.shape[1] - len(blocks) * rows)
        part = jnp.dot(split, onehot(ref[start : start + trees, :]), preferred_element_type=F32)
        part = digits_sum(part, top, WIDE)
        if before_ref is not None:
            part = part + before_ref[:, at : at + rows]
        out_ref[:, at : at + rows] = part


def solution(mesh):
    n_row, n_leaf = mesh.shape["row"], mesh.shape["leaf"]
    far_stride, near_stride = n_row // 2, 1
    row_strides = [1 << bit for bit in range(1, n_row.bit_length() - 2)]
    leaf_strides = [1 << bit for bit in range(n_leaf.bit_length() - 1)]
    n_keys = 4
    n_share = n_row // n_keys

    def swap(value, axis, stride):
        size = n_row if axis == "row" else n_leaf
        return lax.ppermute(value, axis, [(i, i ^ stride) for i in range(size)])

    def far_swap(value):
        return swap(value, "row", far_stride)

    def near_swap(value):
        return swap(value, "row", near_stride)

    def half_sum(value, axis, strides):
        for stride in strides[:-1]:
            value = value + swap(value, axis, stride)
        return value, swap(value, axis, strides[-1])

    def leaf_sum(value, cut):
        for stride in leaf_strides[:-1]:
            value = value + swap(value, "leaf", stride)
        parts = value[:, :cut], value[:, cut:]
        return [(v, swap(v, "leaf", leaf_strides[-1])) for v in parts]

    def per_device(leaf_index, targets):
        width = targets.shape[1] // n_keys
        rows, trees = leaf_index.shape
        half = trees // 2
        columns, span = half * LEAVES, n_keys * rows
        cut = span // 2
        scale = (LEAVES / (rows * n_row)) ** 0.5
        flops = 2 * columns * rows * 256
        row = lax.axis_index("row")
        key = (row // far_stride) * 2 + row % 2
        share_stride = row_strides[-1]
        share = (row // share_stride) % 2
        core = lax.axis_index("leaf") % 2
        place = jnp.stack([key, key ^ 1, key ^ 2, key ^ 3, share, key ^ (2 + core)]).astype(jnp.int32)

        def share_of(first, second, tail=None):
            value = jnp.where(share == 0, first, second)
            return value if tail is None else jnp.concatenate([value, tail], 1)

        def share_swap(value):
            return swap(value, "row", share_stride)

        def gather(value):
            m = 2 * columns
            tail = value[:, m:] if value.shape[1] > m else None
            far = far_swap(share_of(value[:, :columns], value[:, columns:m], tail))
            near = near_swap(value)
            both = near_swap(far)
            other = share_swap(jnp.concatenate([far[:, :columns], both[:, :columns]], 0))
            return [value, near, far, both, other]

        def pack(place_ref, target_ref, own_ref, near_ref, far_ref):
            chunk = lambda m: target_ref[pl.ds(pl.multiple_of(place_ref[m] * width, width), width), :]
            own_ref[...] = chunk(0)
            near_ref[...] = chunk(1)
            far_ref[...] = chunk(5)

        own = leaf_index.T
        t_own, t_near, t_far = pl.pallas_call(
            pack,
            out_shape=(array(width, rows), array(width, rows), array(width, rows)),
            in_specs=[pl.BlockSpec(memory_space=pltpu.SMEM), VMEM],
            out_specs=(VMEM, VMEM, VMEM),
            compiler_params=pltpu.CompilerParams(vmem_limit_bytes=VMEM_LIMIT),
            name="pack",
        )(place, targets.T)
        far = [far_swap(own[:half]), far_swap(own[half:])]
        t_mine = far_swap(t_far)
        t_near = near_swap(t_near)
        t_theirs = swap(t_mine, "leaf", 1)
        t_far, t_relay = (jnp.where(core == c, t_mine, t_theirs) for c in range(2))
        near = near_swap(own)
        both = [near_swap(far[0]), near_swap(far[1])]
        t_both = near_swap(t_relay)

        def leaves_of(h):
            return own, near, far[h], both[h]

        def blocks_of(refs, h):
            return tuple((ref, start, half) for ref, start in zip(refs, (h * half, h * half, 0, 0)))

        split_two = pltpu.VMEM((NARROW[1] * width, 2 * rows), F8)
        split_one = pltpu.VMEM((NARROW[1] * width, rows), F8)

        def back0_own(own_ref, near_ref, first_ref, second_ref, out0_ref, out1_ref, split_ref):
            chunks = first_ref[...], second_ref[...]
            top = jnp.maximum(top_of(chunks[0]), top_of(chunks[1]))
            for index, chunk in enumerate(chunks):
                split_ref[:, index * rows : (index + 1) * rows] = digits_of(chunk, top, NARROW)
            for h, ref in enumerate((out0_ref, out1_ref)):
                ref[...] = spread(blocks_of((own_ref, near_ref), h), split_ref, top, scale)

        def back0_far(far0_ref, far1_ref, value_ref, in0_ref, in1_ref, out0_ref, out1_ref, split_ref):
            value = value_ref[...]
            top = top_of(value)
            split_ref[...] = digits_of(value, top, NARROW)
            out0_ref[...] = in0_ref[...] + spread(((far0_ref, 0, half),), split_ref, top, scale)
            out1_ref[...] = in1_ref[...] + spread(((far1_ref, 0, half),), split_ref, top, scale)

        def back0_both(leaf_ref, value_ref, in_ref, out_ref, split_ref):
            value = value_ref[...]
            top = top_of(value)
            split_ref[...] = digits_of(value, top, NARROW)
            out_ref[...] = in_ref[...] + spread(((leaf_ref, 0, half),), split_ref, top, scale)

        b_half = array(width, columns)
        parts = call(back0_own, (b_half, b_half), [split_two], 4 * flops, own, near, t_own, t_near)
        parts = call(back0_far, (b_half, b_half), [split_one], 2 * flops, *far, t_far, *parts)
        pairs = []
        for h in range(2):
            part = call(back0_both, b_half, [split_one], flops, both[h], t_both, parts[h])
            pairs.append(half_sum(part, "row", row_strides))

        w_shape = array(width, span + LANES)

        def forward0_first(l0, l1, l2, l3, mine_ref, theirs_ref, out_ref, base_ref):
            base = mine_ref[...] + theirs_ref[...]
            base_ref[...] = base
            collect(blocks_of((l0, l1, l2, l3), 0), base, out_ref, None)
            out_ref[:, cut : cut + LANES] = lane_sums(base * base)

        def forward0_second(l0, l1, l2, l3, mine_ref, theirs_ref, in_ref, first_ref, out_ref, base_ref):
            base = mine_ref[...] + theirs_ref[...]
            base_ref[:, :columns] = first_ref[...]
            base_ref[:, columns:] = base
            collect(blocks_of((l0, l1, l2, l3), 1), base, out_ref, in_ref)
            tail = slice(cut, cut + LANES)
            out_ref[:, tail] = in_ref[:, tail] + lane_sums(base * base)

        part, first = call(forward0_first, (w_shape, b_half), [], 4 * flops, *leaves_of(0), *pairs[0])
        part, b0 = call(
            forward0_second, (w_shape, array(width, 2 * columns)), [], 4 * flops, *leaves_of(1), *pairs[1], part, first
        )
        w_pairs = leaf_sum(part, cut + LANES)

        def backward_rows0(own_ref, near_ref, mine_ref, theirs_ref, *refs):
            rows_ref, (out0_ref, out1_ref, last_ref, split_ref) = refs[:-4], refs[-4:]
            value = mine_ref[:, :cut] + theirs_ref[:, :cut]
            last_ref[...] = value
            top = top_of(value)
            split_ref[...] = digits_of(value, top, NARROW)
            at = columns
            for other in [value] + [ref[...] for ref in rows_ref]:
                out0_ref[:, at : at + LANES] = (scale * scale) * lane_sums(value * other)
                at += LANES
            out0_ref[:, at:] = (mine_ref[:, cut:] + theirs_ref[:, cut:]) * (1.0 / n_share)
            blocks = (own_ref, near_ref)
            out0_ref[:, :columns] = spread(blocks_of(blocks, 0), split_ref, top, scale * scale)
            out1_ref[...] = spread(blocks_of(blocks, 1), split_ref, top, scale * scale)

        def backward_rows1(far_ref, both_ref, mine_ref, theirs_ref, in_ref, *refs):
            rows_ref, (out_ref, last_ref, split_ref, top_ref) = refs[:-4], refs[-4:]
            value = mine_ref[...] + theirs_ref[...]
            last_ref[...] = value
            top = top_of(value)
            top_ref[...] = top
            split_ref[...] = digits_of(value, top, NARROW)
            at = columns
            for other in [value] + [ref[...] for ref in rows_ref]:
                found = (scale * scale) * lane_sums(value * other)
                out_ref[:, at : at + LANES] = in_ref[:, at : at + LANES] + found
                at += LANES
            out_ref[:, at:] = in_ref[:, at:]
            blocks = ((far_ref, 0, half), (both_ref, 0, half))
            found = spread(blocks, split_ref, top, scale * scale)
            out_ref[:, :columns] = in_ref[:, :columns] + found

        def backward_last(far_ref, both_ref, split_ref, top_ref, in_ref, out_ref):
            blocks = ((far_ref, 0, half), (both_ref, 0, half))
            out_ref[...] = in_ref[...] + spread(blocks, split_ref, top_ref[...], scale * scale)

        def backward(w_pairs, extra, rows_before=((), ())):
            payload, w_half = array(width, columns + extra * LANES), array(width, cut)
            part0, part1, last0 = call(
                backward_rows0,
                (payload, b_half, w_half),
                [split_two],
                4 * flops,
                own,
                near,
                *w_pairs[0],
                *rows_before[0],
            )
            part0, last1, split, top = call(
                backward_rows1,
                (payload, w_half, jax.ShapeDtypeStruct((NARROW[1] * width, cut), F8), array(width, 1)),
                [],
                2 * flops,
                far[0],
                both[0],
                *w_pairs[1],
                part0,
                *rows_before[1],
            )
            pairs = [half_sum(part0, "row", row_strides)]
            part1 = call(backward_last, b_half, [], 2 * flops, far[1], both[1], split, top, part1)
            return pairs + [half_sum(part1, "row", row_strides)], ((last0,), (last1,))

        pairs, w0 = backward(w_pairs, 2)

        def step_of(norm, curve):
            return jnp.where(norm > 0.0, norm / (curve + ridge_weight * norm), 1.0)

        def scalar(value):
            return jnp.sum(value, axis=(0, 1), keepdims=True)

        def theta_of(tail):
            return step_of(scalar(tail[:, LANES:]), scalar(tail[:, :LANES]))

        def residual(base, mine_ref, theirs_ref, theta):
            image = mine_ref[:, :columns] + theirs_ref[:, :columns]
            return base - theta * (image + ridge_weight * base)

        def forward1_first(l0, l1, l2, l3, mine_ref, theirs_ref, base_ref, out_ref, res_ref):
            tail = mine_ref[:, columns:] + theirs_ref[:, columns:]
            base = base_ref[:, :columns]
            res = residual(base, mine_ref, theirs_ref, theta_of(tail))
            res_ref[:, :columns] = res
            res_ref[:, columns:] = tail
            collect(blocks_of((l0, l1, l2, l3), 0), res, out_ref, None)
            out_ref[:, cut : cut + LANES] = lane_sums(res * res)
            out_ref[:, cut + LANES : cut + 2 * LANES] = lane_sums(res * base)

        def forward1_second(
            l0, l1, l2, l3, mine_ref, theirs_ref, base_ref, in_ref, first_ref, out_ref, res_ref
        ):
            tail = first_ref[:, columns:]
            base = base_ref[:, columns:]
            res = residual(base, mine_ref, theirs_ref, theta_of(tail))
            res_ref[:, :columns] = first_ref[:, :columns]
            res_ref[:, columns : 2 * columns] = res
            res_ref[:, 2 * columns :] = tail
            collect(blocks_of((l0, l1, l2, l3), 1), res, out_ref, in_ref)
            for index, other in enumerate((res, base)):
                tail = slice(cut + index * LANES, cut + (index + 1) * LANES)
                out_ref[:, tail] = in_ref[:, tail] + lane_sums(res * other)

        w_shape = array(width, span + 2 * LANES)
        part, first = call(
            forward1_first, (w_shape, array(width, columns + 2 * LANES)), [], 4 * flops, *leaves_of(0), *pairs[0], b0
        )
        part, res = call(
            forward1_second,
            (w_shape, array(width, 2 * columns + 2 * LANES)),
            [],
            4 * flops,
            *leaves_of(1),
            *pairs[1],
            b0,
            part,
            first,
        )
        w_pairs = leaf_sum(part, cut + 2 * LANES)

        pairs, _ = backward(w_pairs, 4, w0)
        b2 = [mine + theirs for mine, theirs in pairs]

        def combine(place_ref, *refs):
            base, res = refs[:5], refs[5:10]
            (image0, near0, image1, near1, far2, both2, z_far2, z_both2) = refs[10:18]
            solution_ref, residual_ref = refs[18:]

            def tail(ref, start, at):
                return scalar(ref[:, start + at * LANES : start + (at + 1) * LANES])

            keys = range(n_keys)
            starts = (2 * columns, 2 * columns, columns, columns)
            b = [tail(res[m], starts[m], 0) for m in keys]
            a = [tail(res[m], starts[m], 1) for m in keys]
            tails = (image0, near0, far2, both2)
            e, f, c, d = ([tail(tails[m], columns, at) for m in keys] for at in range(4))
            norm0 = sum(a)
            alpha0 = norm0 / (sum(b) + ridge_weight * norm0)
            theta = [step_of(a[m], b[m]) for m in keys]
            rho = [alpha0 / theta[m] for m in keys]
            square = lambda x, y, xx, xy, yy: x * x * xx + 2.0 * x * y * xy + y * y * yy
            norm1 = sum(square(rho[m], 1.0 - rho[m], c[m], d[m], a[m]) for m in keys)
            beta = norm1 / norm0
            other = [1.0 - rho[m] + beta for m in keys]
            curve = sum(
                square(rho[m], other[m], e[m], f[m], b[m])
                + ridge_weight * square(rho[m], other[m], c[m], d[m], a[m])
                for m in keys
            )
            alpha1 = norm1 / curve

            def finish(m, at_columns, v0, v1, v2):
                at = pl.ds(pl.multiple_of(place_ref[m] * width, width), width)
                solution_ref[at, at_columns] = (alpha0 + alpha1 * other[m]) * v0 + (alpha1 * rho[m]) * v1
                residual_ref[at, at_columns] = (
                    ((1.0 - rho[m]) - alpha1 * other[m] / theta[m]) * v0
                    + (rho[m] + alpha1 * (other[m] / theta[m] - ridge_weight * rho[m])) * v1
                    - (alpha1 * rho[m]) * v2
                )

            for m, images in enumerate(((image0, image1), (near0, near1))):
                for h in range(2):
                    at = slice(h * columns, (h + 1) * columns)
                    finish(m, at, base[m][:, at], res[m][:, at], images[h][:, :columns])
            mine = pl.ds(pl.multiple_of(place_ref[4] * columns, columns), columns)
            theirs = pl.ds(pl.multiple_of((1 - place_ref[4]) * columns, columns), columns)
            for m, image, z_image in ((2, far2, z_far2), (3, both2, z_both2)):
                finish(m, mine, base[m][:, :columns], res[m][:, :columns], image[:, :columns])
                z = slice((m - 2) * width, (m - 1) * width)
                finish(m, theirs, base[4][z, :], res[4][z, :], z_image[...])

        far = share_of(b2[0][:, :columns], b2[1], b2[0][:, columns:])
        far = far_swap(far)
        nears = near_swap(b2[0]), near_swap(b2[1])
        z_far = share_swap(far[:, :columns])
        both = near_swap(far)
        z_both = share_swap(both[:, :columns])
        out = array(n_keys * width, 2 * columns)
        parts = (*gather(b0), *gather(res), b2[0], nears[0], b2[1], nears[1], far, both, z_far, z_both)
        result = pl.pallas_call(
            combine,
            out_shape=(out, out),
            in_specs=[pl.BlockSpec(memory_space=pltpu.SMEM)] + [VMEM] * len(parts),
            out_specs=(VMEM, VMEM),
            compiler_params=pltpu.CompilerParams(vmem_limit_bytes=VMEM_LIMIT),
            name="combine",
        )(place, *parts)
        return tuple(value.T for value in result)

    return jax.shard_map(
        per_device,
        mesh=mesh,
        in_specs=(P("row", "leaf"), P("row", None)),
        out_specs=(P("leaf", None), P("leaf", None)),
        check_vma=False,
    )
```
